512 devices in a mesh: grp: 16 (over z, y_lo), ep: 32 (over x, y_hi, core).
Axes of the slice: x: 4, y: 8 (y_hi: 4, y_lo: 2; y = y_hi * 2 + y_lo), z: 8, core: 2. Of those that a mesh axis runs over, the one named last changes fastest.
Arguments:
- tokens: bfloat16 [65536, 2048], P(('grp', 'ep')), may hold values from -6 to 6
- norm_gain: float32 [2048], replicated, may hold values from 0.25 to 1.75
- w_gate: bfloat16 [32, 2048, 512], P('ep', 'grp'), may hold values from -0.125 to 0.125
- w_up: bfloat16 [32, 2048, 512], P('ep', 'grp'), may hold values from -0.125 to 0.125
- w_down: bfloat16 [32, 512, 2048], P('ep', None, 'grp'), may hold values from -0.25 to 0.25
- expert_ids: int32 [65536, 2], P(('grp', 'ep')), may hold values from 0 to 31, all different within a row; in each aligned block of 128 rows (0 to 127, 128 to 255, ...) at most 12 rows name the same one
- probs: float32 [65536, 2], P(('grp', 'ep')), may hold values from 0.1 to 1
- out_grad: bfloat16 [65536, 2048], P(('grp', 'ep')), may hold values from -6 to 6
Outputs:
- grad_tokens: bfloat16 [65536, 2048], P(('grp', 'ep'))
- grad_up: float32 [32, 2048, 512], P('ep', 'grp')
- grad_down: float32 [32, 512, 2048], P('ep', None, 'grp')
The draws below stay inside these ranges and needn't reach their ends.
Inputs may be any that keep to these rules, and one draw needn't show every extreme that they name: `expert_ids`: each row names 2 different experts; among the 128 rows of one device, no expert is named by more than 12 rows, a bound that some block reaches.
All inputs are finite; a program needn't handle non-finite values.
Results may differ from the reference program's by a relative error of at most 0.017.
Values may be sent and summed in bfloat16 or wider, within the bound.
No kernel may reach another device: no remote copies, remote signals or barrier semaphores. Data moves between devices by JAX's collectives and lax.ppermute only.
A program may use at most 64 MiB of HBM per device.

```python
import math
import jax
import jax.numpy as jnp
import numpy as np
from jax import lax

D = 2048
F = 512
K = 2
TOK_DEV = 128
EXPERTS = 32
CAP = 12
TOKENS = 65536
N_GRP = 16
N_EP = 32


def levels(stream_key, shape, pieces, least, largest):
    level, own = 1.0, jax.random.fold_in(stream_key, 6)
    for position, shards_of in pieces:
        draws = jnp.exp(jax.random.uniform(jax.random.fold_in(own, position), (shards_of,), jnp.float32, least / len(pieces), largest / len(pieces)))
        level = level * jnp.repeat(draws, shape[position] // shards_of).reshape([-1 if axis == position else 1 for axis in range(len(shape))])
    return level


def shared_out(own_key, own, number, rows, amount, top, most, lean):
    sequence = jax.random.permutation(own_key, amount)
    heavy_load, common = shares(amount, rows * top, most, lean, True), shares(amount, rows * top, most, lean, False)
    places = jnp.arange(amount)

    def named(lengths, turn):
        used = int((lengths > 0).sum())
        fixed = max(1, used // 4)
        shifted = fixed + (places - fixed + turn * (used - fixed)) % max(1, amount - fixed)
        return jnp.zeros((amount,), jnp.int32).at[sequence[jnp.where(places < fixed, places, shifted)]].set(jnp.asarray(lengths, jnp.int32))

    lengths = jnp.where(number % 4 == 0, named(heavy_load, number // 4), named(common, number - number // 4 - 1))
    mixed = jax.random.permutation(jax.random.fold_in(own, 3), amount)
    giver, receiver = mixed[0:amount // 2 * 2:2], mixed[1:amount // 2 * 2:2]
    margin = jnp.minimum(lengths[giver] - 1, most - lengths[receiver]) // 2
    margin = jnp.where((giver == sequence[0]) | (receiver == sequence[0]) | (lengths[receiver] == 0), 0, jnp.maximum(margin, 0))
    shifted = jax.random.randint(jax.random.fold_in(own, 4), (amount // 2,), 0, 1 << 20) % (margin + 1)
    lengths = lengths.at[giver].add(-shifted).at[receiver].add(shifted)
    labels = jnp.searchsorted(jnp.cumsum(lengths), jnp.arange(rows * top), side="right").astype(jnp.int32)
    listing = labels.reshape(top, rows).T
    listing = listing[jax.random.permutation(jax.random.fold_in(own, 1), rows)]
    turn = jax.random.randint(jax.random.fold_in(own, 2), (rows, 1), 0, top)
    return jnp.take_along_axis(listing, (jnp.arange(top)[None, :] + turn) % top, axis=1)


def shares(amount, total, reach, slope, full):
    loads = [(1 << 20) // math.isqrt(standing ** slope) + 1 for standing in range(1, amount + 1)]
    largest = reach if full else min(reach, max(-(-total // amount), total * loads[0] // sum(loads)))
    least = 1 if total - largest >= amount - 1 else 0
    given, spare = [largest] + [least] * (amount - 1), total - largest - least * (amount - 1)
    while spare > 0:
        free = [i for i in range(1, amount) if given[i] < largest] or [i for i in range(1, amount) if given[i] < reach]
        mass, budget = sum([loads[i] for i in free]), spare
        for i in free:
            addition = min(reach - given[i], max(1, budget * loads[i] // mass), spare)
            given[i] = given[i] + addition
            spare = spare - addition
    return np.array(given)


def scatter_about(key, shape, spread, bound, shards=(), kind=jnp.bfloat16):
    loudness = levels(key, shape, shards, -0.22, 0.18) if shards else 1.0
    drawn = jax.random.normal(key, shape, jnp.float32) * spread * loudness
    return jnp.minimum(jnp.maximum(drawn, -bound), bound).astype(kind)


def setup_inputs(seed: int = 0) -> dict:
    arg_keys = jax.random.split(jax.random.key(seed), 9)
    tokens = scatter_about(arg_keys[0], (TOKENS, D), 1.0, 6.0, ((0, 512),))
    norm_gain = jnp.clip(1.0 + 0.15 * jax.random.normal(arg_keys[1], (D,), jnp.float32), 0.25, 1.75)
    w_gate = scatter_about(arg_keys[2], (EXPERTS, D, F), D ** -0.5, 0.125, ((0, 32), (1, 16)))
    w_up = scatter_about(arg_keys[3], (EXPERTS, D, F), D ** -0.5, 0.125, ((0, 32), (1, 16)))
    w_down = scatter_about(arg_keys[4], (EXPERTS, F, D), F ** -0.5, 0.25, ((0, 32), (2, 16)))
    expert_ids_keys = jax.random.split(jax.random.fold_in(arg_keys[5], 1), TOKENS // TOK_DEV)
    expert_ids_turns = jax.random.permutation(jax.random.fold_in(arg_keys[5], 3), TOKENS // TOK_DEV)
    expert_ids = jax.vmap(lambda own, number: shared_out(jax.random.fold_in(arg_keys[5], 2), own, number, TOK_DEV, EXPERTS, K, CAP, 2))(expert_ids_keys, expert_ids_turns).reshape((TOKENS, K))
    probs = jnp.clip(jnp.exp(math.log(1.0) - 2.3025851 * jax.random.uniform(arg_keys[6], (TOKENS, K), jnp.float32) ** levels(arg_keys[6], (TOKENS, K), ((0, 512),), -0.2, 0.2)), 0.1, 1.0)
    out_grad = scatter_about(arg_keys[7], (TOKENS, D), 1.0, 6.0, ((0, 512),))
    return {"tokens": tokens, "norm_gain": norm_gain, "w_gate": w_gate, "w_up": w_up, "w_down": w_down, "expert_ids": expert_ids, "probs": probs, "out_grad": out_grad}


EPS = 1e-06

def expert_pass(hidden_rows, cot_rows, gate_full, up_full, down_full):
    hidden_f = hidden_rows.astype(jnp.float32)
    cot_f = cot_rows.astype(jnp.float32)
    gate_f = gate_full.astype(jnp.float32)
    up_f = up_full.astype(jnp.float32)
    pre_gate = jnp.dot(hidden_f, gate_f)
    pre_up = jnp.dot(hidden_f, up_f)
    sigmoid_gate = jax.nn.sigmoid(pre_gate)
    act_gate = pre_gate * sigmoid_gate
    swiglu = (act_gate * pre_up).astype(jnp.bfloat16)
    d_swiglu = jnp.dot(cot_f, down_full.astype(jnp.float32).T)
    d_up_pre = (d_swiglu * act_gate).astype(jnp.bfloat16)
    d_gate_pre = (d_swiglu * pre_up * sigmoid_gate * (1.0 + pre_gate * (1.0 - sigmoid_gate))).astype(jnp.bfloat16)
    d_hidden = (jnp.dot(d_gate_pre.astype(jnp.float32), gate_f.T) + jnp.dot(d_up_pre.astype(jnp.float32), up_f.T)).astype(jnp.bfloat16)
    part_up = jnp.dot(hidden_f.T, d_up_pre.astype(jnp.float32))
    part_down = jnp.dot(swiglu.astype(jnp.float32).T, cot_f)
    return (d_hidden, part_up, part_down)

def reference(tokens, norm_gain, w_gate, w_up, w_down, expert_ids, probs, out_grad):
    token_f = tokens.astype(jnp.float32)
    inverse = lax.rsqrt(lax.optimization_barrier(jnp.mean(token_f * token_f, axis=1, keepdims=True)) + EPS)
    normed = token_f * inverse
    hidden = (normed * norm_gain[None, :]).astype(jnp.bfloat16)
    cot_full = out_grad.astype(jnp.float32)
    top_count = expert_ids.shape[1]
    group_rows = N_EP * TOK_DEV
    slot_count = N_EP * CAP
    width = tokens.shape[1]

    def per_expert(d_normed, expert):
        gate_full = w_gate[expert]
        up_full = w_up[expert]
        down_full = w_down[expert]

        def per_group(carry, group):
            d_acc, sum_up, sum_down = carry
            start = (group * group_rows).astype(jnp.int32)
            ids_group = lax.dynamic_slice_in_dim(expert_ids, start, group_rows, 0).reshape(-1)
            match = ids_group == expert
            flat_index = jnp.nonzero(match, size=slot_count, fill_value=0)[0].astype(jnp.int32)
            count = jnp.sum(match.astype(jnp.int32))
            valid = jnp.arange(slot_count, dtype=jnp.int32) < count
            global_row = start + flat_index // top_count
            which = flat_index % top_count
            hidden_rows = jnp.where(valid[:, None], hidden[global_row], jnp.zeros((), jnp.bfloat16)).astype(jnp.bfloat16)
            weight_rows = probs[global_row, which]
            cot_rows = (weight_rows[:, None] * cot_full[global_row]).astype(jnp.bfloat16)
            cot_rows = jnp.where(valid[:, None], cot_rows, jnp.zeros((), jnp.bfloat16)).astype(jnp.bfloat16)
            d_hidden, part_up, part_down = expert_pass(hidden_rows, cot_rows, gate_full, up_full, down_full)
            added = jnp.where(valid[:, None], d_hidden.astype(jnp.float32), jnp.zeros((), jnp.float32))
            d_acc = d_acc.at[global_row].add(added)
            sum_up = sum_up + lax.optimization_barrier(part_up.astype(jnp.bfloat16)).astype(jnp.float32)
            sum_down = sum_down + lax.optimization_barrier(part_down.astype(jnp.bfloat16)).astype(jnp.float32)
            return ((d_acc, sum_up, sum_down), None)
        first = (d_normed, jnp.zeros((width, F), jnp.float32), jnp.zeros((F, width), jnp.float32))
        (d_normed, sum_up, sum_down), _ = lax.scan(per_group, first, jnp.arange(N_GRP, dtype=jnp.int32))
        return (d_normed, (sum_up, sum_down))
    d_start = jnp.zeros(tokens.shape, jnp.float32)
    d_normed, (all_up, all_down) = lax.scan(per_expert, d_start, jnp.arange(EXPERTS, dtype=jnp.int32))
    factor = 1.0 / math.sqrt(TOKENS * top_count / EXPERTS)
    d_scaled = d_normed * norm_gain[None, :]
    dot_mean = lax.optimization_barrier(jnp.mean(d_scaled * normed, axis=1, keepdims=True))
    grad_tokens = (inverse * (d_scaled - normed * dot_mean)).astype(jnp.bfloat16)
    return (grad_tokens, all_up * factor, all_down * factor)
```

```python
import math

import jax
import jax.numpy as jnp
from jax import lax
from jax.experimental import pallas as pl
from jax.experimental.pallas import tpu as pltpu
from jax.sharding import PartitionSpec as P

EPS = 1e-06
BF = jnp.bfloat16
F32 = jnp.float32


RING = 8
PAIR = 2
LOW = 8
HALF = 4


def shift_z(value, step):
    pairs = [
        (z * PAIR + y, ((z + step) % RING) * PAIR + y) for z in range(RING) for y in range(PAIR)
    ]
    return lax.ppermute(value, "grp", pairs)


def swap_y(value):
    pairs = [(z * PAIR + y, z * PAIR + 1 - y) for z in range(RING) for y in range(PAIR)]
    return lax.ppermute(value, "grp", pairs)


def dot(left, right, dims):
    return lax.dot_general(left, right, (dims, ((), ())), preferred_element_type=F32)


def dispatch_kernel(tokens, gain, ids, probs, out_grad, send, select):
    rows, width = tokens.shape
    experts = send.shape[0] // LOW
    token_f = tokens[...].astype(F32)
    inverse = lax.rsqrt(jnp.mean(token_f * token_f, axis=1, keepdims=True) + EPS)
    hidden = (token_f * inverse * gain[...]).astype(BF)
    expert = lax.broadcasted_iota(jnp.int32, (experts, rows), 0)
    first, second = ids[0:1, :] == expert, ids[1:2, :] == expert
    routed = jnp.where(first | second, 1.0, 0.0)
    weight = jnp.where(first, probs[0:1, :], 0.0) + jnp.where(second, probs[1:2, :], 0.0)
    earlier = lax.broadcasted_iota(jnp.int32, (rows, rows), 0) < lax.broadcasted_iota(
        jnp.int32, (rows, rows), 1
    )
    rank = dot(routed.astype(BF), jnp.where(earlier, 1.0, 0.0).astype(BF), ((1,), (0,)))
    slot = jnp.where(routed > 0.5, rank, -1.0)
    slot = jnp.broadcast_to(slot[:, None, :], (experts, LOW, rows))
    weight = jnp.broadcast_to(weight[:, None, :], (experts, LOW, rows))
    place = lax.broadcasted_iota(jnp.int32, (experts, LOW, rows), 1)
    low = jnp.where(slot == place.astype(F32), 1.0, 0.0)
    wanted = jnp.where(place < HALF, place + LOW, place + HALF).astype(F32)
    high = jnp.where(slot == wanted, 1.0, 0.0)
    flat = (experts * LOW, rows)
    low_scale = jnp.sum((low * weight).reshape(flat), axis=1, keepdims=True)
    high_scale = jnp.sum(
        jnp.where(place < HALF, high, high * weight).reshape(flat), axis=1, keepdims=True
    )
    low = low.reshape(flat).astype(BF)
    high_left = jnp.where(place < HALF, high, 0.0).reshape(flat).astype(BF)
    high_right = jnp.where(place < HALF, 0.0, high).reshape(flat).astype(BF)
    select[:, 0:rows] = low
    select[:, rows : 2 * rows] = high_left
    select[:, 2 * rows : 3 * rows] = high_right
    take = ((1,), (0,))
    send[:, 0:width] = dot(low, hidden, take).astype(BF)
    send[:, width : 2 * width] = (dot(low, out_grad[...], take) * low_scale).astype(BF)
    mixed = dot(high_left, hidden, take) + dot(high_right, out_grad[...], take)
    send[:, 2 * width : 3 * width] = (mixed * high_scale).astype(BF)


def turn(value):
    rows, width = value.shape
    value = value.reshape(rows // LOW, LOW, width)
    return pltpu.roll(value, HALF, 1).reshape(rows, width)


def expert_kernel(recv, weights, back, parts):
    rows = recv.shape[0]
    width = recv.shape[1] // 3
    inner = weights.shape[1] // 3
    upper = lax.broadcasted_iota(jnp.int32, (rows, inner), 0) % LOW < HALF
    low_h, low_c, mixed = (recv[:, i * width : (i + 1) * width] for i in range(3))
    row_col = ((1,), (0,))
    col_col = ((1,), (1,))
    row_row = ((0,), (0,))

    def grads(pre_gate, pre_up, d_swiglu):
        sigmoid = jax.nn.sigmoid(pre_gate)
        act = pre_gate * sigmoid
        d_gate = d_swiglu * pre_up * sigmoid * (1.0 + pre_gate * (1.0 - sigmoid))
        return act * pre_up, d_gate, d_swiglu * act

    gate, up, down = (weights[:, i * inner : (i + 1) * inner] for i in range(3))
    swiglu, d_gate, d_up = grads(
        dot(low_h, gate, row_col), dot(low_h, up, row_col), dot(low_c, down, row_col)
    )
    swiglu_x, d_gate_x, d_up_x = grads(
        dot(mixed, gate, row_col), dot(mixed, up, row_col), turn(dot(mixed, down, row_col))
    )
    swiglu_x, d_gate_x, d_up_x = (jnp.where(upper, v, 0.0) for v in (swiglu_x, d_gate_x, d_up_x))
    d_up_b = d_up.astype(BF)
    parts[:, 0:inner] = (
        dot(low_h, d_up_b, row_row) + dot(mixed, d_up_x.astype(BF), row_row)
    ).astype(BF)
    parts[:, inner : 2 * inner] = (
        dot(low_c, swiglu.astype(BF), row_row) + dot(mixed, turn(swiglu_x).astype(BF), row_row)
    ).astype(BF)
    d_gate_b = d_gate.astype(BF)
    back[:, 0:width] = (dot(d_gate_b, gate, col_col) + dot(d_up_b, up, col_col)).astype(BF)
    d_gate_b = (d_gate_x + turn(d_gate_x)).astype(BF)
    d_up_b = (d_up_x + turn(d_up_x)).astype(BF)
    half = width // 2
    left = dot(d_gate_b, gate[:half], col_col) + dot(d_up_b, up[:half], col_col)
    right = dot(d_gate_b, gate[half:], col_col) + dot(d_up_b, up[half:], col_col)
    pick = lax.broadcasted_iota(jnp.int32, (rows, half), 0) % LOW < HALF
    back[:, width : width + half] = jnp.where(pick, left, right).astype(BF)


def finish_kernel(tokens, gain, select, back, out):
    rows, width = tokens.shape
    half = width // 2
    token_f = tokens[...].astype(F32)
    inverse = lax.rsqrt(jnp.mean(token_f * token_f, axis=1, keepdims=True) + EPS)
    normed = token_f * inverse
    low, left, right = (select[:, i * rows : (i + 1) * rows] for i in range(3))
    row_row = ((0,), (0,))
    high = back[:, width : width + half]
    d_normed = dot(low, back[:, 0:width], row_row) + jnp.concatenate(
        [dot(left, high, row_row), dot(right, high, row_row)], axis=1
    )
    scaled = d_normed * gain[...]
    mean = jnp.mean(scaled * normed, axis=1, keepdims=True)
    out[...] = (inverse * (scaled - normed * mean)).astype(BF)


def gather_weights(shard):
    rows, width = shard.shape
    index = lax.axis_index("grp")
    z, y = index // PAIR, index % PAIR
    whole = jnp.zeros((RING * PAIR * rows, width), BF)

    def put(whole, block, step, other):
        spot = (((z + step) % RING) * PAIR + (y + other) % PAIR) * rows
        return lax.dynamic_update_slice(whole, block, (spot, 0))

    chains = []
    partner = swap_y(shard)
    for other, block in ((0, shard), (1, partner)):
        whole = put(whole, block, 0, other)
        chains.append([block, block])
    middle = RING // 2
    for step in range(1, middle + 1):
        for other in range(PAIR):
            for way, sign in ((0, 1), (1, -1)):
                if step == middle and way != other:
                    continue
                chains[other][way] = shift_z(chains[other][way], sign)
                whole = put(whole, chains[other][way], -sign * step, other)
    return whole


def scatter_parts(parts):
    rows = parts.shape[0] // (RING * PAIR)
    width = parts.shape[1]
    index = lax.axis_index("grp")
    z, y = index // PAIR, index % PAIR

    def take(step, other):
        spot = (((z + step) % RING) * PAIR + (y + other) % PAIR) * rows
        return lax.dynamic_slice(parts, (spot, 0), (rows, width))

    def add(left, right):
        return left.astype(F32) + right.astype(F32)

    middle = RING // 2
    chains = {}
    for step in range(middle, 0, -1):
        for other in (1, 0):
            for way, sign in ((0, 1), (1, -1)):
                if step == middle and way != other:
                    continue
                held = chains.get((other, way))
                block = take(sign * step, other)
                if held is not None:
                    block = add(block, held).astype(BF)
                chains[other, way] = shift_z(block, sign)
    away = add(add(take(0, 1), chains[1, 0]), chains[1, 1]).astype(BF)
    mine = add(add(take(0, 0), chains[0, 0]), chains[0, 1])
    return mine + swap_y(away).astype(F32)


def shards(tokens, norm_gain, w_gate, w_up, w_down, expert_ids, probs, out_grad):
    rows, width = tokens.shape
    inner = w_gate.shape[2]
    experts = lax.axis_size("ep")
    shard = jnp.concatenate([w_gate[0], w_up[0], w_down[0].T], axis=1)
    weights = gather_weights(shard)
    gain = norm_gain.reshape(1, width)
    send, select = pl.pallas_call(
        dispatch_kernel,
        out_shape=(
            jax.ShapeDtypeStruct((experts * LOW, 3 * width), BF),
            jax.ShapeDtypeStruct((experts * LOW, 3 * rows), BF),
        ),
        name="dispatch",
    )(tokens, gain, expert_ids.T, probs.T, out_grad)
    recv = lax.all_to_all(
        send.reshape(experts, LOW, 3 * width), "ep", split_axis=0, concat_axis=0, tiled=True
    ).reshape(experts * LOW, 3 * width)
    back, parts = pl.pallas_call(
        expert_kernel,
        out_shape=(
            jax.ShapeDtypeStruct((experts * LOW, width + width // 2), BF),
            jax.ShapeDtypeStruct((width, 2 * inner), BF),
        ),
        name="expert",
    )(recv, weights)
    back = lax.all_to_all(
        back.reshape(experts, LOW, width + width // 2), "ep", split_axis=0, concat_axis=0, tiled=True
    ).reshape(experts * LOW, width + width // 2)
    summed = scatter_parts(parts)
    grad_tokens = pl.pallas_call(
        finish_kernel, out_shape=jax.ShapeDtypeStruct((rows, width), BF), name="finish"
    )(tokens, gain, select, back)
    factor = 1.0 / math.sqrt(
        rows * lax.axis_size("grp") * experts * expert_ids.shape[1] / experts
    )
    summed = summed * factor
    return (grad_tokens, summed[:, :inner][None], summed[:, inner:].T[None])


def solution(mesh):
    in_specs = (
        P(("grp", "ep"), None),
        P(),
        P("ep", "grp", None),
        P("ep", "grp", None),
        P("ep", None, "grp"),
        P(("grp", "ep"), None),
        P(("grp", "ep"), None),
        P(("grp", "ep"), None),
    )
    out_specs = (P(("grp", "ep"), None), P("ep", "grp", None), P("ep", None, "grp"))
    return jax.shard_map(shards, mesh=mesh, in_specs=in_specs, out_specs=out_specs, check_vma=False)
```

```python
import functools
import math

import jax
import jax.numpy as jnp
from jax import lax
from jax.experimental import pallas as pl
from jax.experimental.pallas import tpu as pltpu
from jax.sharding import PartitionSpec as P


EPS = 1e-06
BF = jnp.bfloat16
F32 = jnp.float32


RING = 8
PAIR = 2
LOW = 8
HALF = 4


def shift_z(value, step):
    pairs = [
        (z * PAIR + y, ((z + step) % RING) * PAIR + y) for z in range(RING) for y in range(PAIR)
    ]
    return lax.ppermute(value, "grp", pairs)


def swap_y(value):
    pairs = [(z * PAIR + y, z * PAIR + 1 - y) for z in range(RING) for y in range(PAIR)]
    return lax.ppermute(value, "grp", pairs)


def near(*values):
    return [pltpu.with_memory_space_constraint(value, pltpu.VMEM) for value in values]


def far(*values):
    return [pltpu.with_memory_space_constraint(value, pltpu.HBM) for value in values]


def limit(mebibytes):
    return pltpu.CompilerParams(vmem_limit_bytes=mebibytes << 20)


def spot(index, step, other, rows):
    z, y = index >> 1, index & 1
    place = (((z + step) & (RING - 1)) << 1) | ((y + other) & (PAIR - 1))
    return pl.ds(pl.multiple_of(place * rows, rows), rows)


def dot(left, right, dims):
    return lax.dot_general(left, right, (dims, ((), ())), preferred_element_type=F32)


def dispatch_kernel(
    tokens, gain, ids, probs, out_grad, gate, up, down, send, select, shard
):
    rows, width = tokens.shape
    inner = gate.shape[1]
    shard[:, 0:inner] = gate[...]
    shard[:, inner : 2 * inner] = up[...]
    shard[:, 2 * inner : 3 * inner] = down[...].T
    experts = send.shape[0] // LOW
    token_f = tokens[...].astype(F32)
    inverse = lax.rsqrt(jnp.mean(token_f * token_f, axis=1, keepdims=True) + EPS)
    hidden = (token_f * inverse * gain[...]).astype(BF)
    expert = lax.broadcasted_iota(jnp.int32, (experts, rows), 0)
    first, second = ids[0:1, :] == expert, ids[1:2, :] == expert
    routed = jnp.where(first | second, 1.0, 0.0)
    weight = jnp.where(first, probs[0:1, :], 0.0) + jnp.where(second, probs[1:2, :], 0.0)
    earlier = lax.broadcasted_iota(jnp.int32, (rows, rows), 0) < lax.broadcasted_iota(
        jnp.int32, (rows, rows), 1
    )
    rank = dot(routed.astype(BF), jnp.where(earlier, 1.0, 0.0).astype(BF), ((1,), (0,)))
    slot = jnp.where(routed > 0.5, rank, -1.0)
    slot = jnp.broadcast_to(slot[:, None, :], (experts, LOW, rows))
    weight = jnp.broadcast_to(weight[:, None, :], (experts, LOW, rows))
    place = lax.broadcasted_iota(jnp.int32, (experts, LOW, rows), 1)
    low = jnp.where(slot == place.astype(F32), 1.0, 0.0)
    wanted = jnp.where(place < HALF, place + LOW, place + HALF).astype(F32)
    high = jnp.where(slot == wanted, 1.0, 0.0)
    flat = (experts * LOW, rows)
    low_scale = jnp.sum((low * weight).reshape(flat), axis=1, keepdims=True)
    high_scale = jnp.sum(
        jnp.where(place < HALF, high, high * weight).reshape(flat), axis=1, keepdims=True
    )
    low = low.reshape(flat).astype(BF)
    high_left = jnp.where(place < HALF, high, 0.0).reshape(flat).astype(BF)
    high_right = jnp.where(place < HALF, 0.0, high).reshape(flat).astype(BF)
    select[:, 0:rows] = low
    select[:, rows : 2 * rows] = high_left
    select[:, 2 * rows : 3 * rows] = high_right
    take = ((1,), (0,))
    send[:, 0:width] = dot(low, hidden, take).astype(BF)
    send[:, width : 2 * width] = (dot(low, out_grad[...], take) * low_scale).astype(BF)
    mixed = dot(high_left, hidden, take) + dot(high_right, out_grad[...], take)
    send[:, 2 * width : 3 * width] = (mixed * high_scale).astype(BF)


def turn(value):
    rows, width = value.shape
    value = value.reshape(rows // LOW, LOW, width)
    return pltpu.roll(value, HALF, 1).reshape(rows, width)


def expert_kernel(places, where, recv, *refs):
    count = len(places)
    blocks, refs = refs[:count], refs[count:]
    grad_pre, both, pieces, (last, parts, sems) = refs[0], refs[1], refs[2:-3], refs[-3:]
    rows = recv.shape[0]
    width = recv.shape[1] // 3
    inner = last.shape[1]
    index = where[0]
    block_rows = blocks[0].shape[0]
    copies = []
    for third in range(3):
        target = last if third == 2 else both.at[:, third * inner : (third + 1) * inner]
        copies.append([])
        for i, (step, other) in enumerate(places):
            copies[third].append(
                pltpu.make_async_copy(
                    blocks[i].at[:, third * inner : (third + 1) * inner],
                    target.at[spot(index, step, other, block_rows), :],
                    sems.at[third * count + i],
                )
            )
            copies[third][i].start()

    def arrived(third):
        for copy in copies[third]:
            copy.wait()

    upper = lax.broadcasted_iota(jnp.int32, (rows, inner), 0) % LOW < HALF
    low_h, low_c, mixed = (recv[:, i * width : (i + 1) * width] for i in range(3))
    row_col = ((1,), (0,))
    row_row = ((0,), (0,))

    def grads(pre_gate, pre_up, d_swiglu):
        sigmoid = jax.nn.sigmoid(pre_gate)
        act = pre_gate * sigmoid
        d_gate = d_swiglu * pre_up * sigmoid * (1.0 + pre_gate * (1.0 - sigmoid))
        return act * pre_up, d_gate, d_swiglu * act

    arrived(0)
    gate = both[:, 0:inner]
    pre_gate, pre_gate_x = dot(low_h, gate, row_col), dot(mixed, gate, row_col)
    arrived(1)
    up = both[:, inner : 2 * inner]
    pre_up, pre_up_x = dot(low_h, up, row_col), dot(mixed, up, row_col)
    arrived(2)
    down = last[...]
    d_swiglu, d_swiglu_x = dot(low_c, down, row_col), turn(dot(mixed, down, row_col))
    swiglu, d_gate, d_up = grads(pre_gate, pre_up, d_swiglu)
    swiglu_x, d_gate_x, d_up_x = grads(pre_gate_x, pre_up_x, d_swiglu_x)
    swiglu_x, d_gate_x, d_up_x = (jnp.where(upper, v, 0.0) for v in (swiglu_x, d_gate_x, d_up_x))
    d_up_b = d_up.astype(BF)
    parts[:, 0:inner] = (
        dot(low_h, d_up_b, row_row) + dot(mixed, d_up_x.astype(BF), row_row)
    ).astype(BF)
    parts[:, inner : 2 * inner] = (
        dot(low_c, swiglu.astype(BF), row_row) + dot(mixed, turn(swiglu_x).astype(BF), row_row)
    ).astype(BF)
    for i, value in enumerate((d_gate, d_up, d_gate_x + turn(d_gate_x), d_up_x + turn(d_up_x))):
        grad_pre[:, i * inner : (i + 1) * inner] = value.astype(BF)
    for (step, other), piece in zip(places, pieces, strict=True):
        piece[...] = parts[spot(index, step, other, block_rows), :]


def back_kernel(grad_pre, weights, back):
    rows = grad_pre.shape[0]
    width, both = weights.shape
    half = width // 2
    col_col = ((1,), (1,))
    back[:, 0:width] = dot(grad_pre[:, 0:both], weights[:, 0:both], col_col).astype(BF)
    high = grad_pre[:, both : 2 * both]
    left = dot(high, weights[0:half, 0:both], col_col)
    right = dot(high, weights[half:width, 0:both], col_col)
    pick = lax.broadcasted_iota(jnp.int32, (rows, half), 0) % LOW < HALF
    back[:, width : width + half] = jnp.where(pick, left, right).astype(BF)


def finish_kernel(tokens, gain, select, back, out):
    rows, width = tokens.shape
    half = width // 2
    token_f = tokens[...].astype(F32)
    inverse = lax.rsqrt(jnp.mean(token_f * token_f, axis=1, keepdims=True) + EPS)
    normed = token_f * inverse
    low, left, right = (select[:, i * rows : (i + 1) * rows] for i in range(3))
    row_row = ((0,), (0,))
    high = back[:, width : width + half]
    d_normed = dot(low, back[:, 0:width], row_row) + jnp.concatenate(
        [dot(left, high, row_row), dot(right, high, row_row)], axis=1
    )
    scaled = d_normed * gain[...]
    mean = jnp.mean(scaled * normed, axis=1, keepdims=True)
    out[...] = (inverse * (scaled - normed * mean)).astype(BF)


def last_kernel(factor, piece, first, second, away, grad_up, grad_down):
    inner = grad_up.shape[1]
    total = piece[...].astype(F32) + first[...].astype(F32) + second[...].astype(F32)
    total = (total + away[...].astype(F32)) * factor
    grad_up[...] = total[:, 0:inner]
    grad_down[...] = total[:, inner : 2 * inner].T


def gather_weights(shard):
    partner = swap_y(shard)
    found = {(0, 0): shard, (0, 1): partner}
    chains = [[shard, shard], [partner, partner]]
    middle = RING // 2
    for step in range(1, middle + 1):
        for other in range(PAIR):
            for way, sign in ((0, 1), (1, -1)):
                if step == middle and way != other:
                    continue
                chains[other][way] = shift_z(chains[other][way], sign)
                key = -sign * step if step < middle else middle
                found[key, other] = chains[other][way]
    return found


def scatter_parts(pieces, factor):
    rows, width = pieces[0, 0].shape
    inner = width // 2

    def add(*values):
        total = values[0].astype(F32)
        for value in values[1:]:
            total = total + value.astype(F32)
        return total.astype(BF)

    middle = RING // 2
    chains = {}
    for step in range(middle, 0, -1):
        for other in (1, 0):
            for way, sign in ((0, 1), (1, -1)):
                if step == middle and way != other:
                    continue
                block = pieces[sign * step if step < middle else middle, other]
                if (other, way) in chains:
                    block = add(block, chains[other, way])
                chains[other, way] = shift_z(block, sign)
    away = add(pieces[0, 1], chains[1, 0], chains[1, 1])
    away = swap_y(away)
    return pl.pallas_call(
        functools.partial(last_kernel, factor),
        out_shape=(
            jax.ShapeDtypeStruct((rows, inner), F32),
            jax.ShapeDtypeStruct((inner, rows), F32),
        ),
        compiler_params=limit(8),
        name="last",
    )(*near(pieces[0, 0], chains[0, 0], chains[0, 1], away))


def body(tokens, norm_gain, w_gate, w_up, w_down, expert_ids, probs, out_grad):
    rows, width = tokens.shape
    inner = w_gate.shape[2]
    experts = lax.axis_size("ep")
    gain = norm_gain.reshape(1, width)
    send, select, shard = pl.pallas_call(
        dispatch_kernel,
        out_shape=(
            jax.ShapeDtypeStruct((experts * LOW, 3 * width), BF),
            jax.ShapeDtypeStruct((experts * LOW, 3 * rows), BF),
            jax.ShapeDtypeStruct((rows, 3 * inner), BF),
        ),
        name="dispatch",
    )(tokens, gain, expert_ids.T, probs.T, out_grad, w_gate[0], w_up[0], w_down[0])
    found = gather_weights(shard)
    recv = lax.all_to_all(
        send.reshape(experts, LOW, 3 * width), "ep", split_axis=0, concat_axis=0, tiled=True
    ).reshape(experts * LOW, 3 * width)
    where = lax.axis_index("grp").astype(jnp.int32).reshape(1)
    places = tuple(found)
    grad_pre, both, *pieces = pl.pallas_call(
        functools.partial(expert_kernel, places),
        out_shape=[
            pltpu.VMEM((experts * LOW, 4 * inner), BF),
            pltpu.VMEM((width, 2 * inner), BF),
        ]
        + [pltpu.VMEM((rows, 2 * inner), BF)] * len(places),
        in_specs=[pl.BlockSpec(memory_space=pltpu.SMEM), pl.BlockSpec()]
        + [pl.BlockSpec(memory_space=pltpu.HBM)] * len(places),
        scratch_shapes=[
            pltpu.VMEM((width, inner), BF),
            pltpu.VMEM((width, 2 * inner), BF),
            pltpu.SemaphoreType.DMA((3 * len(places),)),
        ],
        compiler_params=limit(28),
        name="expert",
    )(where, *near(recv), *far(*found.values()))
    pieces = dict(zip(places, pieces, strict=True))
    back = pl.pallas_call(
        back_kernel,
        out_shape=jax.ShapeDtypeStruct((experts * LOW, width + width // 2), BF),
        compiler_params=limit(16),
        name="back",
    )(*near(grad_pre, both))
    back = lax.all_to_all(
        back.reshape(experts, LOW, width + width // 2),
        "ep",
        split_axis=0,
        concat_axis=0,
        tiled=True,
    ).reshape(experts * LOW, width + width // 2)
    factor = 1.0 / math.sqrt(
        rows * lax.axis_size("grp") * experts * expert_ids.shape[1] / experts
    )
    grad_up, grad_down = scatter_parts(pieces, factor)
    grad_tokens = pl.pallas_call(
        finish_kernel,
        out_shape=jax.ShapeDtypeStruct((rows, width), BF),
        compiler_params=limit(20),
        name="finish",
    )(tokens, gain, select, *near(back))
    return (grad_tokens, grad_up[None], grad_down[None])


def solution(mesh):
    in_specs = (
        P(("grp", "ep"), None),
        P(),
        P("ep", "grp", None),
        P("ep", "grp", None),
        P("ep", None, "grp"),
        P(("grp", "ep"), None),
        P(("grp", "ep"), None),
        P(("grp", "ep"), None),
    )
    out_specs = (P(("grp", "ep"), None), P("ep", "grp", None), P("ep", None, "grp"))
    return jax.shard_map(body, mesh=mesh, in_specs=in_specs, out_specs=out_specs, check_vma=False)
```

```python
import functools
import math

import jax
import jax.numpy as jnp
from jax import lax
from jax.experimental import pallas as pl
from jax.experimental.pallas import tpu as pltpu
from jax.sharding import PartitionSpec as P


EPS = 1e-06
BF = jnp.bfloat16
F32 = jnp.float32


RING = 8
PAIR = 2
LOW = 8
HALF = 4


def shift_z(value, step):
    pairs = [
        (z * PAIR + y, ((z + step) % RING) * PAIR + y) for z in range(RING) for y in range(PAIR)
    ]
    return lax.ppermute(value, "grp", pairs)


def swap_y(value):
    pairs = [(z * PAIR + y, z * PAIR + 1 - y) for z in range(RING) for y in range(PAIR)]
    return lax.ppermute(value, "grp", pairs)


def near(*values):
    return [pltpu.with_memory_space_constraint(value, pltpu.VMEM) for value in values]


def far(*values):
    return [pltpu.with_memory_space_constraint(value, pltpu.HBM) for value in values]


def limit(mebibytes):
    return pltpu.CompilerParams(vmem_limit_bytes=mebibytes << 20)


def spot(index, step, other, rows):
    z, y = index >> 1, index & 1
    place = (((z + step) & (RING - 1)) << 1) | ((y + other) & (PAIR - 1))
    return pl.ds(pl.multiple_of(place * rows, rows), rows)


def dot(left, right, dims):
    return lax.dot_general(left, right, (dims, ((), ())), preferred_element_type=F32)


def dispatch_kernel(*refs):
    fars, (send_far, select_far, shard_far) = refs[:8], refs[8:11]
    tokens, gain, ids, probs, out_grad, turned, send, select, shard, sems = refs[11:]
    rows, width = tokens.shape
    inner = turned.shape[0]
    homes = (tokens, gain, ids, probs, out_grad)
    homes += (shard.at[:, 0:inner], shard.at[:, inner : 2 * inner], turned)
    loads = [
        pltpu.make_async_copy(source, target, sems.at[i])
        for i, (source, target) in enumerate(zip(fars, homes, strict=True))
    ]
    for i in (0, 2, 3, 1, 4, 7, 5, 6):
        loads[i].start()
    stores = []

    def ship(source, target):
        stores.append(pltpu.make_async_copy(source, target, sems.at[8 + len(stores)]))
        stores[-1].start()

    def ship_third(third):
        here = slice(third * width, (third + 1) * width)
        ship(send.at[:, here], send_far.at[:, here])

    experts = send.shape[0] // LOW
    for i in (0, 1, 2, 3):
        loads[i].wait()
    token_f = tokens[...].astype(F32)
    inverse = lax.rsqrt(jnp.mean(token_f * token_f, axis=1, keepdims=True) + EPS)
    hidden = (token_f * inverse * gain[...]).astype(BF)
    expert = lax.broadcasted_iota(jnp.int32, (experts, rows), 0)
    first, second = ids[0:1, :] == expert, ids[1:2, :] == expert
    routed = jnp.where(first | second, 1.0, 0.0)
    weight = jnp.where(first, probs[0:1, :], 0.0) + jnp.where(second, probs[1:2, :], 0.0)
    earlier = lax.broadcasted_iota(jnp.int32, (rows, rows), 0) < lax.broadcasted_iota(
        jnp.int32, (rows, rows), 1
    )
    rank = dot(routed.astype(BF), jnp.where(earlier, 1.0, 0.0).astype(BF), ((1,), (0,)))
    slot = jnp.where(routed > 0.5, rank, -1.0)
    slot = jnp.broadcast_to(slot[:, None, :], (experts, LOW, rows))
    weight = jnp.broadcast_to(weight[:, None, :], (experts, LOW, rows))
    place = lax.broadcasted_iota(jnp.int32, (experts, LOW, rows), 1)
    low = jnp.where(slot == place.astype(F32), 1.0, 0.0)
    wanted = jnp.where(place < HALF, place + LOW, place + HALF).astype(F32)
    high = jnp.where(slot == wanted, 1.0, 0.0)
    flat = (experts * LOW, rows)
    low_scale = jnp.sum((low * weight).reshape(flat), axis=1, keepdims=True)
    high_scale = jnp.sum(
        jnp.where(place < HALF, high, high * weight).reshape(flat), axis=1, keepdims=True
    )
    low = low.reshape(flat).astype(BF)
    high_left = jnp.where(place < HALF, high, 0.0).reshape(flat).astype(BF)
    high_right = jnp.where(place < HALF, 0.0, high).reshape(flat).astype(BF)
    select[:, 0:rows] = low
    select[:, rows : 2 * rows] = high_left
    select[:, 2 * rows : 3 * rows] = high_right
    take = ((1,), (0,))
    send[:, 0:width] = dot(low, hidden, take).astype(BF)
    ship_third(0)
    loads[4].wait()
    send[:, width : 2 * width] = (dot(low, out_grad[...], take) * low_scale).astype(BF)
    ship_third(1)
    mixed = dot(high_left, hidden, take) + dot(high_right, out_grad[...], take)
    send[:, 2 * width : 3 * width] = (mixed * high_scale).astype(BF)
    ship_third(2)
    for i in (5, 6, 7):
        loads[i].wait()
    shard[:, 2 * inner : 3 * inner] = turned[...].T
    ship(shard, shard_far)
    ship(select, select_far)
    for copy in stores:
        copy.wait()


def turn(value):
    rows, width = value.shape
    value = value.reshape(rows // LOW, LOW, width)
    return pltpu.roll(value, HALF, 1).reshape(rows, width)


def expert_kernel(places, where, recv, *refs):
    count = len(places)
    blocks, refs = refs[:count], refs[count:]
    grad_pre, both, pieces, (last, parts, sems) = refs[0], refs[1], refs[2:-3], refs[-3:]
    rows = recv.shape[0]
    width = recv.shape[1] // 3
    inner = last.shape[1]
    index = where[0]
    block_rows = blocks[0].shape[0]
    copies = []
    for third in range(3):
        target = last if third == 2 else both.at[:, third * inner : (third + 1) * inner]
        copies.append([])
        for i, (step, other) in enumerate(places):
            copies[third].append(
                pltpu.make_async_copy(
                    blocks[i].at[:, third * inner : (third + 1) * inner],
                    target.at[spot(index, step, other, block_rows), :],
                    sems.at[third * count + i],
                )
            )
            copies[third][i].start()

    def arrived(third):
        for copy in copies[third]:
            copy.wait()

    upper = lax.broadcasted_iota(jnp.int32, (rows, inner), 0) % LOW < HALF
    low_h, low_c, mixed = (recv[:, i * width : (i + 1) * width] for i in range(3))
    row_col = ((1,), (0,))
    row_row = ((0,), (0,))

    def grads(pre_gate, pre_up, d_swiglu):
        sigmoid = jax.nn.sigmoid(pre_gate)
        act = pre_gate * sigmoid
        d_gate = d_swiglu * pre_up * sigmoid * (1.0 + pre_gate * (1.0 - sigmoid))
        return act * pre_up, d_gate, d_swiglu * act

    arrived(0)
    gate = both[:, 0:inner]
    pre_gate, pre_gate_x = dot(low_h, gate, row_col), dot(mixed, gate, row_col)
    arrived(1)
    up = both[:, inner : 2 * inner]
    pre_up, pre_up_x = dot(low_h, up, row_col), dot(mixed, up, row_col)
    arrived(2)
    down = last[...]
    d_swiglu, d_swiglu_x = dot(low_c, down, row_col), turn(dot(mixed, down, row_col))
    swiglu, d_gate, d_up = grads(pre_gate, pre_up, d_swiglu)
    swiglu_x, d_gate_x, d_up_x = grads(pre_gate_x, pre_up_x, d_swiglu_x)
    swiglu_x, d_gate_x, d_up_x = (jnp.where(upper, v, 0.0) for v in (swiglu_x, d_gate_x, d_up_x))
    d_up_b = d_up.astype(BF)
    parts[:, 0:inner] = (
        dot(low_h, d_up_b, row_row) + dot(mixed, d_up_x.astype(BF), row_row)
    ).astype(BF)
    parts[:, inner : 2 * inner] = (
        dot(low_c, swiglu.astype(BF), row_row) + dot(mixed, turn(swiglu_x).astype(BF), row_row)
    ).astype(BF)
    for i, value in enumerate((d_gate, d_up, d_gate_x + turn(d_gate_x), d_up_x + turn(d_up_x))):
        grad_pre[:, i * inner : (i + 1) * inner] = value.astype(BF)
    for (step, other), piece in zip(places, pieces, strict=True):
        piece[...] = parts[spot(index, step, other, block_rows), :]


def back_kernel(grad_pre, weights, back):
    rows = grad_pre.shape[0]
    width, both = weights.shape
    half = width // 2
    col_col = ((1,), (1,))
    back[:, 0:width] = dot(grad_pre[:, 0:both], weights[:, 0:both], col_col).astype(BF)
    high = grad_pre[:, both : 2 * both]
    left = dot(high, weights[0:half, 0:both], col_col)
    right = dot(high, weights[half:width, 0:both], col_col)
    pick = lax.broadcasted_iota(jnp.int32, (rows, half), 0) % LOW < HALF
    back[:, width : width + half] = jnp.where(pick, left, right).astype(BF)


def finish_kernel(tokens, gain, select, back, out):
    rows, width = tokens.shape
    half = width // 2
    token_f = tokens[...].astype(F32)
    inverse = lax.rsqrt(jnp.mean(token_f * token_f, axis=1, keepdims=True) + EPS)
    normed = token_f * inverse
    low, left, right = (select[:, i * rows : (i + 1) * rows] for i in range(3))
    row_row = ((0,), (0,))
    high = back[:, width : width + half]
    d_normed = dot(low, back[:, 0:width], row_row) + jnp.concatenate(
        [dot(left, high, row_row), dot(right, high, row_row)], axis=1
    )
    scaled = d_normed * gain[...]
    mean = jnp.mean(scaled * normed, axis=1, keepdims=True)
    out[...] = (inverse * (scaled - normed * mean)).astype(BF)


def add_kernel(*refs):
    total = refs[0][...].astype(F32)
    for held in refs[1:-1]:
        total = total + held[...].astype(F32)
    refs[-1][...] = total.astype(BF)


def mine_kernel(piece, first, second, total):
    total[...] = piece[...].astype(F32) + first[...].astype(F32) + second[...].astype(F32)


def last_kernel(factor, mine, away, grad_up, grad_down):
    inner = grad_up.shape[1]
    grad_up[...] = (mine[:, 0:inner] + away[:, 0:inner].astype(F32)) * factor
    right = (mine[:, inner : 2 * inner] + away[:, inner : 2 * inner].astype(F32)) * factor
    grad_down[...] = right.T


def gather_weights(shard):
    partner = swap_y(shard)
    found = {(0, 0): shard, (0, 1): partner}
    chains = [[shard, shard], [partner, partner]]
    middle = RING // 2
    for step in range(1, middle + 1):
        for other in range(PAIR):
            for way, sign in ((0, 1), (1, -1)):
                if step == middle and way != other:
                    continue
                chains[other][way] = shift_z(chains[other][way], sign)
                key = -sign * step if step < middle else middle
                found[key, other] = chains[other][way]
    return found


def scatter_parts(pieces, factor):
    rows, width = pieces[0, 0].shape
    inner = width // 2

    def add(*values):
        total = values[0].astype(F32)
        for value in values[1:]:
            total = total + value.astype(F32)
        return total.astype(BF)

    def add_near(*values):
        return pl.pallas_call(
            add_kernel,
            out_shape=pltpu.VMEM((rows, width), BF),
            compiler_params=limit(2),
            name="add",
        )(*near(*values))

    middle = RING // 2
    chains = {}
    for step in range(middle, 0, -1):
        for other in (1, 0):
            for way, sign in ((0, 1), (1, -1)):
                if step == middle and way != other:
                    continue
                block = pieces[sign * step if step < middle else middle, other]
                if (other, way) in chains:
                    late = step == 1 or (step == 2 and way == other)
                    block = (add_near if late else add)(block, chains[other, way])
                chains[other, way] = shift_z(block, sign)
    away = add_near(pieces[0, 1], chains[1, 0], chains[1, 1])
    away = swap_y(away)
    mine = pl.pallas_call(
        mine_kernel,
        out_shape=pltpu.VMEM((rows, width), F32),
        compiler_params=limit(2),
        name="mine",
    )(*near(pieces[0, 0], chains[0, 0], chains[0, 1]))
    return pl.pallas_call(
        functools.partial(last_kernel, factor),
        out_shape=(
            jax.ShapeDtypeStruct((rows, inner), F32),
            jax.ShapeDtypeStruct((inner, rows), F32),
        ),
        compiler_params=limit(4),
        name="last",
    )(*near(mine, away))


def body(tokens, norm_gain, w_gate, w_up, w_down, expert_ids, probs, out_grad):
    rows, width = tokens.shape
    inner = w_gate.shape[2]
    experts = lax.axis_size("ep")
    gain = norm_gain.reshape(1, width)
    there = pl.BlockSpec(memory_space=pltpu.HBM)
    send, select, shard = pl.pallas_call(
        dispatch_kernel,
        out_shape=(
            jax.ShapeDtypeStruct((experts * LOW, 3 * width), BF),
            jax.ShapeDtypeStruct((experts * LOW, 3 * rows), BF),
            jax.ShapeDtypeStruct((rows, 3 * inner), BF),
        ),
        in_specs=[there] * 8,
        out_specs=(there, there, there),
        scratch_shapes=[
            pltpu.VMEM((rows, width), BF),
            pltpu.VMEM((1, width), F32),
            pltpu.VMEM((2, rows), jnp.int32),
            pltpu.VMEM((2, rows), F32),
            pltpu.VMEM((rows, width), BF),
            pltpu.VMEM((inner, rows), BF),
            pltpu.VMEM((experts * LOW, 3 * width), BF),
            pltpu.VMEM((experts * LOW, 3 * rows), BF),
            pltpu.VMEM((rows, 3 * inner), BF),
            pltpu.SemaphoreType.DMA((13,)),
        ],
        name="dispatch",
    )(*far(tokens, gain, expert_ids.T, probs.T, out_grad, w_gate[0], w_up[0], w_down[0]))
    found = gather_weights(shard)
    recv = lax.all_to_all(
        send.reshape(experts, LOW, 3 * width), "ep", split_axis=0, concat_axis=0, tiled=True
    ).reshape(experts * LOW, 3 * width)
    where = lax.axis_index("grp").astype(jnp.int32).reshape(1)
    places = tuple(found)
    grad_pre, both, *pieces = pl.pallas_call(
        functools.partial(expert_kernel, places),
        out_shape=[
            pltpu.VMEM((experts * LOW, 4 * inner), BF),
            pltpu.VMEM((width, 2 * inner), BF),
        ]
        + [pltpu.VMEM((rows, 2 * inner), BF)] * len(places),
        in_specs=[pl.BlockSpec(memory_space=pltpu.SMEM), pl.BlockSpec()]
        + [pl.BlockSpec(memory_space=pltpu.HBM)] * len(places),
        scratch_shapes=[
            pltpu.VMEM((width, inner), BF),
            pltpu.VMEM((width, 2 * inner), BF),
            pltpu.SemaphoreType.DMA((3 * len(places),)),
        ],
        compiler_params=limit(28),
        name="expert",
    )(where, *near(recv), *far(*found.values()))
    pieces = dict(zip(places, pieces, strict=True))
    back = pl.pallas_call(
        back_kernel,
        out_shape=jax.ShapeDtypeStruct((experts * LOW, width + width // 2), BF),
        compiler_params=limit(16),
        name="back",
    )(*near(grad_pre, both))
    back = lax.all_to_all(
        back.reshape(experts, LOW, width + width // 2),
        "ep",
        split_axis=0,
        concat_axis=0,
        tiled=True,
    ).reshape(experts * LOW, width + width // 2)
    factor = 1.0 / math.sqrt(
        rows * lax.axis_size("grp") * experts * expert_ids.shape[1] / experts
    )
    grad_up, grad_down = scatter_parts(pieces, factor)
    grad_tokens = pl.pallas_call(
        finish_kernel,
        out_shape=jax.ShapeDtypeStruct((rows, width), BF),
        compiler_params=limit(20),
        name="finish",
    )(tokens, gain, select, *near(back))
    return (grad_tokens, grad_up[None], grad_down[None])


def solution(mesh):
    in_specs = (
        P(("grp", "ep"), None),
        P(),
        P("ep", "grp", None),
        P("ep", "grp", None),
        P("ep", None, "grp"),
        P(("grp", "ep"), None),
        P(("grp", "ep"), None),
        P(("grp", "ep"), None),
    )
    out_specs = (P(("grp", "ep"), None), P("ep", "grp", None), P("ep", None, "grp"))
    return jax.shard_map(body, mesh=mesh, in_specs=in_specs, out_specs=out_specs, check_vma=False)
```

```python
import functools
import math

import jax
import jax.numpy as jnp
from jax import lax
from jax.experimental import pallas as pl
from jax.experimental.pallas import tpu as pltpu
from jax.sharding import PartitionSpec as P


EPS = 1e-06
BF = jnp.bfloat16
F32 = jnp.float32


RING = 8
PAIR = 2
LOW = 8
HALF = 4


def shift_z(value, step):
    pairs = [
        (z * PAIR + y, ((z + step) % RING) * PAIR + y) for z in range(RING) for y in range(PAIR)
    ]
    return lax.ppermute(value, "grp", pairs)


def swap_y(value):
    pairs = [(z * PAIR + y, z * PAIR + 1 - y) for z in range(RING) for y in range(PAIR)]
    return lax.ppermute(value, "grp", pairs)


def near(*values):
    return [pltpu.with_memory_space_constraint(value, pltpu.VMEM) for value in values]


def far(*values):
    return [pltpu.with_memory_space_constraint(value, pltpu.HBM) for value in values]


def limit(mebibytes):
    return pltpu.CompilerParams(vmem_limit_bytes=mebibytes << 20)


def spot(index, step, other, rows):
    z, y = index >> 1, index & 1
    place = (((z + step) & (RING - 1)) << 1) | ((y + other) & (PAIR - 1))
    return pl.ds(pl.multiple_of(place * rows, rows), rows)


def dot(left, right, dims):
    return lax.dot_general(left, right, (dims, ((), ())), preferred_element_type=F32)


def dispatch_kernel(*refs):
    fars, (send_far, select_far, shard_far) = refs[:8], refs[8:11]
    tokens, gain, ids, probs, out_grad, turned, send, select, shard, sems = refs[11:]
    rows, width = tokens.shape
    inner = turned.shape[0]
    homes = (tokens, gain, ids, probs, out_grad)
    homes += (shard.at[:, 0:inner], shard.at[:, inner : 2 * inner], turned)
    loads = [
        pltpu.make_async_copy(source, target, sems.at[i])
        for i, (source, target) in enumerate(zip(fars, homes, strict=True))
    ]
    for i in (0, 2, 3, 1, 4, 7, 5, 6):
        loads[i].start()
    stores = []

    def ship(source, target):
        stores.append(pltpu.make_async_copy(source, target, sems.at[8 + len(stores)]))
        stores[-1].start()

    def ship_third(third):
        here = slice(third * width, (third + 1) * width)
        ship(send.at[:, here], send_far.at[:, here])

    experts = send.shape[0] // LOW
    for i in (0, 1, 2, 3):
        loads[i].wait()
    token_f = tokens[...].astype(F32)
    inverse = lax.rsqrt(jnp.mean(token_f * token_f, axis=1, keepdims=True) + EPS)
    hidden = (token_f * inverse * gain[...]).astype(BF)
    expert = lax.broadcasted_iota(jnp.int32, (experts, rows), 0)
    first, second = ids[0:1, :] == expert, ids[1:2, :] == expert
    routed = jnp.where(first | second, 1.0, 0.0)
    weight = jnp.where(first, probs[0:1, :], 0.0) + jnp.where(second, probs[1:2, :], 0.0)
    earlier = lax.broadcasted_iota(jnp.int32, (rows, rows), 0) < lax.broadcasted_iota(
        jnp.int32, (rows, rows), 1
    )
    rank = dot(routed.astype(BF), jnp.where(earlier, 1.0, 0.0).astype(BF), ((1,), (0,)))
    slot = jnp.where(routed > 0.5, rank, -1.0)
    slot = jnp.broadcast_to(slot[:, None, :], (experts, LOW, rows))
    weight = jnp.broadcast_to(weight[:, None, :], (experts, LOW, rows))
    place = lax.broadcasted_iota(jnp.int32, (experts, LOW, rows), 1)
    low = jnp.where(slot == place.astype(F32), 1.0, 0.0)
    wanted = jnp.where(place < HALF, place + LOW, place + HALF).astype(F32)
    high = jnp.where(slot == wanted, 1.0, 0.0)
    flat = (experts * LOW, rows)
    low_scale = jnp.sum((low * weight).reshape(flat), axis=1, keepdims=True)
    high_scale = jnp.sum(
        jnp.where(place < HALF, high, high * weight).reshape(flat), axis=1, keepdims=True
    )
    low = low.reshape(flat).astype(BF)
    high_left = jnp.where(place < HALF, high, 0.0).reshape(flat).astype(BF)
    high_right = jnp.where(place < HALF, 0.0, high).reshape(flat).astype(BF)
    select[:, 0:rows] = low
    select[:, rows : 2 * rows] = high_left
    select[:, 2 * rows : 3 * rows] = high_right
    take = ((1,), (0,))
    send[:, 0:width] = dot(low, hidden, take).astype(BF)
    ship_third(0)
    loads[4].wait()
    send[:, width : 2 * width] = (dot(low, out_grad[...], take) * low_scale).astype(BF)
    ship_third(1)
    mixed = dot(high_left, hidden, take) + dot(high_right, out_grad[...], take)
    send[:, 2 * width : 3 * width] = (mixed * high_scale).astype(BF)
    ship_third(2)
    for i in (5, 6, 7):
        loads[i].wait()
    shard[:, 2 * inner : 3 * inner] = turned[...].T
    ship(shard, shard_far)
    ship(select, select_far)
    for copy in stores:
        copy.wait()


def turn(value):
    rows, width = value.shape
    value = value.reshape(rows // LOW, LOW, width)
    return pltpu.roll(value, HALF, 1).reshape(rows, width)


def expert_kernel(places, where, recv, *refs):
    count = len(places)
    blocks, refs = refs[:count], refs[count:]
    grad_pre, both, pieces, (last, parts, sems) = refs[0], refs[1], refs[2:-3], refs[-3:]
    rows = recv.shape[0]
    width = recv.shape[1] // 3
    inner = last.shape[1]
    index = where[0]
    block_rows = blocks[0].shape[0]
    copies = []
    for third in range(3):
        target = last if third == 2 else both.at[:, third * inner : (third + 1) * inner]
        copies.append([])
        for i, (step, other) in enumerate(places):
            copies[third].append(
                pltpu.make_async_copy(
                    blocks[i].at[:, third * inner : (third + 1) * inner],
                    target.at[spot(index, step, other, block_rows), :],
                    sems.at[third * count + i],
                )
            )
            copies[third][i].start()

    def arrived(third):
        for copy in copies[third]:
            copy.wait()

    upper = lax.broadcasted_iota(jnp.int32, (rows, inner), 0) % LOW < HALF
    low_h, low_c, mixed = (recv[:, i * width : (i + 1) * width] for i in range(3))
    row_col = ((1,), (0,))
    row_row = ((0,), (0,))

    def grads(pre_gate, pre_up, d_swiglu):
        sigmoid = jax.nn.sigmoid(pre_gate)
        act = pre_gate * sigmoid
        d_gate = d_swiglu * pre_up * sigmoid * (1.0 + pre_gate * (1.0 - sigmoid))
        return act * pre_up, d_gate, d_swiglu * act

    arrived(0)
    gate = both[:, 0:inner]
    pre_gate, pre_gate_x = dot(low_h, gate, row_col), dot(mixed, gate, row_col)
    arrived(1)
    up = both[:, inner : 2 * inner]
    pre_up, pre_up_x = dot(low_h, up, row_col), dot(mixed, up, row_col)
    arrived(2)
    down = last[...]
    d_swiglu, d_swiglu_x = dot(low_c, down, row_col), turn(dot(mixed, down, row_col))
    swiglu, d_gate, d_up = grads(pre_gate, pre_up, d_swiglu)
    swiglu_x, d_gate_x, d_up_x = grads(pre_gate_x, pre_up_x, d_swiglu_x)
    swiglu_x, d_gate_x, d_up_x = (jnp.where(upper, v, 0.0) for v in (swiglu_x, d_gate_x, d_up_x))
    d_up_b = d_up.astype(BF)
    parts[:, 0:inner] = (
        dot(low_h, d_up_b, row_row) + dot(mixed, d_up_x.astype(BF), row_row)
    ).astype(BF)
    parts[:, inner : 2 * inner] = (
        dot(low_c, swiglu.astype(BF), row_row) + dot(mixed, turn(swiglu_x).astype(BF), row_row)
    ).astype(BF)
    for i, value in enumerate((d_gate, d_up, d_gate_x + turn(d_gate_x), d_up_x + turn(d_up_x))):
        grad_pre[:, i * inner : (i + 1) * inner] = value.astype(BF)
    for (step, other), piece in zip(places, pieces, strict=True):
        piece[...] = parts[spot(index, step, other, block_rows), :]


def back_kernel(grad_pre, weights, back_far, back, sems):
    rows = grad_pre.shape[0]
    width, both = weights.shape
    half = width // 2
    col_col = ((1,), (1,))
    stores = []

    def ship(start):
        here = slice(start, start + half)
        stores.append(
            pltpu.make_async_copy(back.at[:, here], back_far.at[:, here], sems.at[len(stores)])
        )
        stores[-1].start()

    high = grad_pre[:, both : 2 * both]
    left = dot(high, weights[0:half, 0:both], col_col)
    right = dot(high, weights[half:width, 0:both], col_col)
    pick = lax.broadcasted_iota(jnp.int32, (rows, half), 0) % LOW < HALF
    back[:, width : width + half] = jnp.where(pick, left, right).astype(BF)
    ship(width)
    for start in (0, half):
        part = dot(grad_pre[:, 0:both], weights[start : start + half, 0:both], col_col)
        back[:, start : start + half] = part.astype(BF)
        ship(start)
    for copy in stores:
        copy.wait()


def finish_kernel(tokens, gain, select, back, out):
    rows, width = tokens.shape
    half = width // 2
    token_f = tokens[...].astype(F32)
    inverse = lax.rsqrt(jnp.mean(token_f * token_f, axis=1, keepdims=True) + EPS)
    normed = token_f * inverse
    low, left, right = (select[:, i * rows : (i + 1) * rows] for i in range(3))
    row_row = ((0,), (0,))
    high = back[:, width : width + half]
    d_normed = dot(low, back[:, 0:width], row_row) + jnp.concatenate(
        [dot(left, high, row_row), dot(right, high, row_row)], axis=1
    )
    scaled = d_normed * gain[...]
    mean = jnp.mean(scaled * normed, axis=1, keepdims=True)
    out[...] = (inverse * (scaled - normed * mean)).astype(BF)


def add_kernel(*refs):
    total = refs[0][...].astype(F32)
    for held in refs[1:-1]:
        total = total + held[...].astype(F32)
    refs[-1][...] = total.astype(BF)


def mine_kernel(piece, first, second, total):
    total[...] = piece[...].astype(F32) + first[...].astype(F32) + second[...].astype(F32)


def last_kernel(factor, mine, away, grad_up, grad_down):
    inner = grad_up.shape[1]
    grad_up[...] = (mine[:, 0:inner] + away[:, 0:inner].astype(F32)) * factor
    right = (mine[:, inner : 2 * inner] + away[:, inner : 2 * inner].astype(F32)) * factor
    grad_down[...] = right.T


def gather_weights(shard):
    partner = swap_y(shard)
    found = {(0, 0): shard, (0, 1): partner}
    chains = [[shard, shard], [partner, partner]]
    middle = RING // 2
    for step in range(1, middle + 1):
        for other in range(PAIR):
            for way, sign in ((0, 1), (1, -1)):
                if step == middle and way != other:
                    continue
                chains[other][way] = shift_z(chains[other][way], sign)
                key = -sign * step if step < middle else middle
                found[key, other] = chains[other][way]
    return found


def scatter_parts(pieces, factor):
    rows, width = pieces[0, 0].shape
    inner = width // 2

    def add(*values):
        total = values[0].astype(F32)
        for value in values[1:]:
            total = total + value.astype(F32)
        return total.astype(BF)

    def add_near(*values):
        return pl.pallas_call(
            add_kernel,
            out_shape=pltpu.VMEM((rows, width), BF),
            compiler_params=limit(2),
            name="add",
        )(*near(*values))

    middle = RING // 2
    chains = {}
    for step in range(middle, 0, -1):
        for other in (1, 0):
            for way, sign in ((0, 1), (1, -1)):
                if step == middle and way != other:
                    continue
                block = pieces[sign * step if step < middle else middle, other]
                if (other, way) in chains:
                    late = step == 1 or (step == 2 and way == other)
                    block = (add_near if late else add)(block, chains[other, way])
                chains[other, way] = shift_z(block, sign)
    away = add_near(pieces[0, 1], chains[1, 0], chains[1, 1])
    away = swap_y(away)
    mine = pl.pallas_call(
        mine_kernel,
        out_shape=pltpu.VMEM((rows, width), F32),
        compiler_params=limit(2),
        name="mine",
    )(*near(pieces[0, 0], chains[0, 0], chains[0, 1]))
    return pl.pallas_call(
        functools.partial(last_kernel, factor),
        out_shape=(
            jax.ShapeDtypeStruct((rows, inner), F32),
            jax.ShapeDtypeStruct((inner, rows), F32),
        ),
        compiler_params=limit(4),
        name="last",
    )(*near(mine, away))


def body(tokens, norm_gain, w_gate, w_up, w_down, expert_ids, probs, out_grad):
    rows, width = tokens.shape
    inner = w_gate.shape[2]
    experts = lax.axis_size("ep")
    gain = norm_gain.reshape(1, width)
    there = pl.BlockSpec(memory_space=pltpu.HBM)
    send, select, shard = pl.pallas_call(
        dispatch_kernel,
        out_shape=(
            jax.ShapeDtypeStruct((experts * LOW, 3 * width), BF),
            jax.ShapeDtypeStruct((experts * LOW, 3 * rows), BF),
            jax.ShapeDtypeStruct((rows, 3 * inner), BF),
        ),
        in_specs=[there] * 8,
        out_specs=(there, there, there),
        scratch_shapes=[
            pltpu.VMEM((rows, width), BF),
            pltpu.VMEM((1, width), F32),
            pltpu.VMEM((2, rows), jnp.int32),
            pltpu.VMEM((2, rows), F32),
            pltpu.VMEM((rows, width), BF),
            pltpu.VMEM((inner, rows), BF),
            pltpu.VMEM((experts * LOW, 3 * width), BF),
            pltpu.VMEM((experts * LOW, 3 * rows), BF),
            pltpu.VMEM((rows, 3 * inner), BF),
            pltpu.SemaphoreType.DMA((13,)),
        ],
        name="dispatch",
    )(*far(tokens, gain, expert_ids.T, probs.T, out_grad, w_gate[0], w_up[0], w_down[0]))
    found = gather_weights(shard)
    recv = lax.all_to_all(
        send.reshape(experts, LOW, 3 * width), "ep", split_axis=0, concat_axis=0, tiled=True
    ).reshape(experts * LOW, 3 * width)
    where = lax.axis_index("grp").astype(jnp.int32).reshape(1)
    places = tuple(found)
    grad_pre, both, *pieces = pl.pallas_call(
        functools.partial(expert_kernel, places),
        out_shape=[
            pltpu.VMEM((experts * LOW, 4 * inner), BF),
            pltpu.VMEM((width, 2 * inner), BF),
        ]
        + [pltpu.VMEM((rows, 2 * inner), BF)] * len(places),
        in_specs=[pl.BlockSpec(memory_space=pltpu.SMEM), pl.BlockSpec()]
        + [pl.BlockSpec(memory_space=pltpu.HBM)] * len(places),
        scratch_shapes=[
            pltpu.VMEM((width, inner), BF),
            pltpu.VMEM((width, 2 * inner), BF),
            pltpu.SemaphoreType.DMA((3 * len(places),)),
        ],
        compiler_params=limit(28),
        name="expert",
    )(where, *near(recv), *far(*found.values()))
    pieces = dict(zip(places, pieces, strict=True))
    back = pl.pallas_call(
        back_kernel,
        out_shape=jax.ShapeDtypeStruct((experts * LOW, width + width // 2), BF),
        out_specs=there,
        scratch_shapes=[
            pltpu.VMEM((experts * LOW, width + width // 2), BF),
            pltpu.SemaphoreType.DMA((3,)),
        ],
        compiler_params=limit(16),
        name="back",
    )(*near(grad_pre, both))
    back = lax.all_to_all(
        back.reshape(experts, LOW, width + width // 2),
        "ep",
        split_axis=0,
        concat_axis=0,
        tiled=True,
    ).reshape(experts * LOW, width + width // 2)
    factor = 1.0 / math.sqrt(
        rows * lax.axis_size("grp") * experts * expert_ids.shape[1] / experts
    )
    grad_up, grad_down = scatter_parts(pieces, factor)
    grad_tokens = pl.pallas_call(
        finish_kernel,
        out_shape=jax.ShapeDtypeStruct((rows, width), BF),
        compiler_params=limit(20),
        name="finish",
    )(tokens, gain, select, *near(back))
    return (grad_tokens, grad_up[None], grad_down[None])


def solution(mesh):
    in_specs = (
        P(("grp", "ep"), None),
        P(),
        P("ep", "grp", None),
        P("ep", "grp", None),
        P("ep", None, "grp"),
        P(("grp", "ep"), None),
        P(("grp", "ep"), None),
        P(("grp", "ep"), None),
    )
    out_specs = (P(("grp", "ep"), None), P("ep", "grp", None), P("ep", None, "grp"))
    return jax.shard_map(body, mesh=mesh, in_specs=in_specs, out_specs=out_specs, check_vma=False)
```
